32 devices in a mesh: chan: 8 (over z, y), tm: 4 (over x, core).
Axes of the slice: x: 2, y: 2, z: 4, core: 2. Of those that a mesh axis runs over, the one named last changes fastest.
Arguments:
- record: bfloat16 [96, 2048], P('chan', 'tm'), may hold values from -6 to 6
- fir: float32 [96, 65], P('chan'), may hold values from -0.75 to 0.75
Outputs:
- xcorr: float32 [4, 96, 96, 256], P('tm', 'chan')
The draws below stay inside these ranges and needn't reach their ends.
All inputs are finite; a program needn't handle non-finite values.
Results may differ from the reference program's by a relative error of at most 0.004.
Values may be sent and summed in bfloat16 or wider, within the bound.
A program may use at most 64 MiB of HBM per device.

```python
import math
import jax
import jax.numpy as jnp
from jax import lax

CHANNELS = 96
GROUP = 512
GROUPS = 4
SAMPLES = 2048
MAXLAG = 128
HALF = 32
TAPS = 65


def steps_of(own_key, dims, pieces, low, largest):
    factor_of, own = 1.0, jax.random.fold_in(own_key, 6)
    for axis_at, blocks in pieces:
        heights = jnp.exp(jax.random.uniform(jax.random.fold_in(own, axis_at), (blocks,), jnp.float32, low / len(pieces), largest / len(pieces)))
        factor_of = factor_of * jnp.repeat(heights, dims[axis_at] // blocks).reshape([-1 if axis == axis_at else 1 for axis in range(len(dims))])
    return factor_of


def gaussian(stream_key, dims, width, most, cuts=(), held_as=jnp.bfloat16):
    factor_of = steps_of(stream_key, dims, cuts, -0.22, 0.18) if cuts else 1.0
    entries = jax.random.normal(stream_key, dims, jnp.float32) * width * factor_of
    return jnp.minimum(jnp.maximum(entries, -most), most).astype(held_as)


def setup_inputs(seed: int = 0) -> dict:
    streams_of = jax.random.split(jax.random.key(seed), 3)
    return {
        "record": gaussian(streams_of[0], (CHANNELS, SAMPLES), 1.0, 6.0, ((0, 8), (1, 4))),
        "fir": gaussian(streams_of[1], (CHANNELS, TAPS), TAPS ** -0.5, 0.75, ((0, 8),), jnp.float32),
    }


def whiten(record, fir):
    widened = jnp.pad(record.astype(jnp.float32), ((0, 0), (HALF, HALF)))
    length = record.shape[1]
    running = jnp.zeros((record.shape[0], length), jnp.float32)
    for k in range(2 * HALF + 1):
        running = running + fir[:, k:k + 1] * widened[:, k:k + length]
    return running.astype(jnp.bfloat16)

def reference(record, fir):
    whitened = whiten(record, fir)
    padded = jnp.pad(whitened.astype(jnp.float32), ((0, 0), (MAXLAG, MAXLAG)))
    span = GROUP + 2 * MAXLAG
    factor = 1.0 / math.sqrt(GROUP)

    def one_group(number):
        offset = (number * GROUP).astype(jnp.int32)
        window = lax.dynamic_slice_in_dim(padded, offset, span, 1)
        leading = window[:, MAXLAG:MAXLAG + GROUP]
        first = jnp.fft.rfft(leading, n=span)
        second = jnp.fft.rfft(window, n=span)
        spectrum = jnp.conj(first)[:, None, :] * second[None, :, :]
        return jnp.fft.irfft(spectrum, n=span)[:, :, :2 * MAXLAG] * factor
    return lax.map(one_group, jnp.arange(GROUPS, dtype=jnp.int32))
```

```python
import math

import jax
import jax.numpy as jnp
from jax import lax
from jax.experimental import pallas as pl
from jax.experimental.pallas import tpu as pltpu
from jax.sharding import PartitionSpec as P

GROUP = 512
MAXLAG = 128
LAGS = 2 * MAXLAG
SPAN = GROUP + LAGS
BAND = GROUP + MAXLAG
HALO = 256
MESH = pl.DeviceIdType.MESH


def whiten(x, fir, first, length):
    taps = fir.shape[1]
    width = -(-(length + taps) // 128) * 128
    x = x[:, first : first + width]
    steps = 8
    moved = [x if b == 0 else pltpu.roll(x, width - b, 1) for b in range(steps)]
    total = None
    for a in range(0, taps, steps):
        part = None
        for b in range(min(steps, taps - a)):
            term = fir[:, a + b : a + b + 1] * moved[b]
            part = term if part is None else part + term
        if a:
            part = pltpu.roll(part, width - a, 1)
        total = part if total is None else total + part
    return total[:, :length]


def gather_kernel(record, fir, gathered, low, high, own, halo_send, halo_recv, send, recv):
    n, tn = lax.axis_size("chan"), lax.axis_size("tm")
    me, tm = lax.axis_index("chan"), lax.axis_index("tm")
    right, left = lax.rem(tm + 1, tn), lax.rem(tm + tn - 1, tn)
    length = record.shape[1]

    barrier = pltpu.get_barrier_semaphore()
    for t in (left, right):
        pl.semaphore_signal(barrier, inc=1, device_id=(me, t), device_id_type=MESH)
    for d in range(1, n):
        pl.semaphore_signal(
            barrier, inc=1, device_id=(lax.rem(me + d, n), tm), device_id_type=MESH
        )
    pl.semaphore_wait(barrier, n + 1)

    to_right = pltpu.make_async_remote_copy(
        record.at[:, length - HALO :], low, halo_send.at[0], halo_recv.at[0],
        device_id=(me, right), device_id_type=MESH,
    )
    to_left = pltpu.make_async_remote_copy(
        record.at[:, :HALO], high, halo_send.at[1], halo_recv.at[1],
        device_id=(me, left), device_id_type=MESH,
    )
    to_right.start()
    to_left.start()
    to_right.wait()
    to_left.wait()

    before = jnp.where(tm > 0, low[...].astype(jnp.float32), 0.0)
    after = jnp.where(tm < tn - 1, high[...].astype(jnp.float32), 0.0)
    x = jnp.concatenate([before, record[...].astype(jnp.float32), after], axis=1)
    half = (fir.shape[1] - 1) // 2
    y = whiten(pltpu.roll(x, x.shape[1] - (HALO - MAXLAG - half), 1), fir[...], 0, SPAN)
    at = lax.broadcasted_iota(jnp.int32, y.shape, 1) + (tm * GROUP - MAXLAG)
    y = jnp.where((at >= 0) & (at < tn * GROUP), y, 0.0).astype(jnp.bfloat16)
    own[...] = y
    gathered[me] = y

    copies = []
    for d in range(1, n):
        copy = pltpu.make_async_remote_copy(
            own, gathered.at[me], send.at[d - 1], recv.at[d - 1],
            device_id=(lax.rem(me + d, n), tm), device_id_type=MESH,
        )
        copy.start()
        copies.append(copy)
    for copy in copies:
        copy.wait()


def correlate_kernel(gathered, out, wide, lead, band, result, sem):
    n, ch = gathered.shape[0], gathered.shape[1]
    rows = n * ch
    me = lax.axis_index("chan")
    factor = 1.0 / math.sqrt(GROUP)
    for c in range(n):
        wide[c * ch : (c + 1) * ch, :] = gathered[c].astype(jnp.float32)
    lead[:, :GROUP] = gathered[me][:, MAXLAG : MAXLAG + GROUP].astype(jnp.float32)
    lead[:, GROUP:] = jnp.zeros((ch, MAXLAG), jnp.float32)
    w = wide[...].astype(jnp.bfloat16)
    both = jnp.concatenate([w[:, :BAND], w[:, MAXLAG:]], axis=0)
    copies = []
    for p in range(ch // 2):
        for s in range(2):
            line = jnp.broadcast_to(lead[2 * p + s : 2 * p + s + 1, :], (MAXLAG, BAND))
            moved = pltpu.roll(line, 0, 1, stride=1, stride_axis=0)
            band[s * MAXLAG : (s + 1) * MAXLAG, :] = moved.astype(jnp.bfloat16)
        r = lax.dot_general(
            both, band[...], (((1,), (1,)), ((), ())), preferred_element_type=jnp.float32
        ) * factor
        for s in range(2):
            for h in range(2):
                result[2 * p + s, :, h * MAXLAG : (h + 1) * MAXLAG] = r[
                    h * rows : (h + 1) * rows, s * MAXLAG : (s + 1) * MAXLAG
                ]
        copy = pltpu.make_async_copy(
            result.at[2 * p : 2 * p + 2], out.at[0, 2 * p : 2 * p + 2], sem.at[p]
        )
        copy.start()
        copies.append(copy)
    for copy in copies:
        copy.wait()


def local(record, fir):
    ch = record.shape[0]
    n = lax.axis_size("chan")
    vmem = pl.BlockSpec(memory_space=pltpu.VMEM)
    gathered = pl.pallas_call(
        gather_kernel,
        out_shape=jax.ShapeDtypeStruct((n, ch, SPAN), jnp.bfloat16),
        in_specs=[vmem, vmem],
        out_specs=vmem,
        scratch_shapes=[
            pltpu.VMEM((ch, HALO), jnp.bfloat16),
            pltpu.VMEM((ch, HALO), jnp.bfloat16),
            pltpu.VMEM((ch, SPAN), jnp.bfloat16),
            pltpu.SemaphoreType.DMA((2,)),
            pltpu.SemaphoreType.DMA((2,)),
            pltpu.SemaphoreType.DMA((n - 1,)),
            pltpu.SemaphoreType.DMA((n - 1,)),
        ],
        compiler_params=pltpu.CompilerParams(collective_id=0, has_side_effects=True),
    )(record, fir)
    return pl.pallas_call(
        correlate_kernel,
        out_shape=jax.ShapeDtypeStruct((1, ch, n * ch, LAGS), jnp.float32),
        in_specs=[vmem],
        out_specs=pl.BlockSpec(memory_space=pl.ANY),
        scratch_shapes=[
            pltpu.VMEM((n * ch, SPAN), jnp.float32),
            pltpu.VMEM((ch, BAND), jnp.float32),
            pltpu.VMEM((2 * MAXLAG, BAND), jnp.bfloat16),
            pltpu.VMEM((ch, n * ch, LAGS), jnp.float32),
            pltpu.SemaphoreType.DMA((ch // 2,)),
        ],
    )(gathered)


def solution(mesh):
    in_specs = (P("chan", "tm"), P("chan", None))
    out_specs = P("tm", "chan", None, None)
    return jax.shard_map(local, mesh=mesh, in_specs=in_specs, out_specs=out_specs, check_vma=False)
```

```python
import math

import jax
import jax.numpy as jnp
from jax import lax
from jax.experimental import pallas as pl
from jax.experimental.pallas import tpu as pltpu
from jax.sharding import PartitionSpec as P

GROUP = 512
MAXLAG = 128
LAGS = 2 * MAXLAG
SPAN = GROUP + LAGS
BAND = GROUP + MAXLAG
HALO = 256
MESH = pl.DeviceIdType.MESH


def whiten(x, fir, first, length):
    taps = fir.shape[1]
    width = -(-(length + taps) // 128) * 128
    x = x[:, first : first + width]
    steps = 8
    moved = [x if b == 0 else pltpu.roll(x, width - b, 1) for b in range(steps)]
    total = None
    for a in range(0, taps, steps):
        part = None
        for b in range(min(steps, taps - a)):
            term = fir[:, a + b : a + b + 1] * moved[b]
            part = term if part is None else part + term
        if a:
            part = pltpu.roll(part, width - a, 1)
        total = part if total is None else total + part
    return total[:, :length]


def pack(y):
    return jnp.concatenate(
        [y[:, k : k + 128] for k in range(0, y.shape[1], 128)], axis=0
    ).astype(jnp.bfloat16)


def gather_kernel(record_hbm, fir_hbm, wide, bands, record, fir, low, high, own, blocks,
                  load, halo_send, halo_recv, send, recv):
    n, tn = lax.axis_size("chan"), lax.axis_size("tm")
    me, tm = lax.axis_index("chan"), lax.axis_index("tm")
    right, left = lax.rem(tm + 1, tn), lax.rem(tm + tn - 1, tn)
    ch, length = record.shape

    barrier = pltpu.get_barrier_semaphore()
    for d in range(n - 1, 0, -1):
        pl.semaphore_signal(
            barrier, inc=1, device_id=(lax.rem(me + d, n), tm), device_id_type=MESH
        )
    for t in (left, right):
        pl.semaphore_signal(barrier, inc=1, device_id=(me, t), device_id_type=MESH)
    get_record = pltpu.make_async_copy(record_hbm, record, load.at[0])
    get_fir = pltpu.make_async_copy(fir_hbm, fir, load.at[1])
    get_record.start()
    get_fir.start()
    get_record.wait()
    get_fir.wait()
    pl.semaphore_wait(barrier, n + 1)

    to_right = pltpu.make_async_remote_copy(
        record.at[:, length - HALO :], low, halo_send.at[0], halo_recv.at[0],
        device_id=(me, right), device_id_type=MESH,
    )
    to_left = pltpu.make_async_remote_copy(
        record.at[:, :HALO], high, halo_send.at[1], halo_recv.at[1],
        device_id=(me, left), device_id_type=MESH,
    )
    to_right.start()
    to_left.start()
    to_right.wait_recv()
    to_left.wait_recv()

    before = jnp.where(tm > 0, low[...].astype(jnp.float32), 0.0)
    after = jnp.where(tm < tn - 1, high[...].astype(jnp.float32), 0.0)
    x = jnp.concatenate([before, record[...].astype(jnp.float32), after], axis=1)
    half = (fir.shape[1] - 1) // 2
    y = whiten(pltpu.roll(x, x.shape[1] - (HALO - MAXLAG - half), 1), fir[...], 0, SPAN)
    at = lax.broadcasted_iota(jnp.int32, y.shape, 1) + (tm * GROUP - MAXLAG)
    y = jnp.where((at >= 0) & (at < tn * GROUP), y, 0.0)
    y = y.astype(jnp.bfloat16).astype(jnp.float32)
    own[...] = pack(y)

    copies = []
    for d in range(1, n):
        copy = pltpu.make_async_remote_copy(
            own, blocks.at[me], send.at[d - 1], recv.at[me],
            device_id=(lax.rem(me + d, n), tm), device_id_type=MESH,
        )
        copy.start()
        copies.append(copy)
    blocks[me] = own[...]

    lead = jnp.concatenate(
        [y[:, MAXLAG : MAXLAG + GROUP], jnp.zeros((ch, MAXLAG), jnp.float32)], axis=1
    )
    for i in range(ch):
        line = jnp.broadcast_to(lead[i : i + 1, :], (MAXLAG, BAND))
        moved = pltpu.roll(line, 0, 1, stride=1, stride_axis=0)
        bands[i * MAXLAG : (i + 1) * MAXLAG, :] = moved.astype(jnp.bfloat16)

    for c in range(n):
        @pl.when(me != c)
        def _():
            pltpu.make_async_remote_copy(
                own, blocks.at[c], send.at[0], recv.at[c],
                device_id=(c, tm), device_id_type=MESH,
            ).wait_recv()

        block = blocks[c].astype(jnp.float32)
        for k in range(SPAN // 128):
            wide[c * ch : (c + 1) * ch, k * 128 : (k + 1) * 128] = block[k * ch : (k + 1) * ch, :]
    to_right.wait_send()
    to_left.wait_send()
    for copy in copies:
        copy.wait_send()


def correlate_kernel(wide, bands, out, result, sem):
    rows = wide.shape[0]
    ch = bands.shape[0] // MAXLAG
    factor = 1.0 / math.sqrt(GROUP)
    w = wide[...].astype(jnp.bfloat16)
    both = jnp.concatenate([w[:, :BAND], w[:, MAXLAG:]], axis=0)
    copies = []
    for p in range(ch // 2):
        r = lax.dot_general(
            both, bands[p * LAGS : (p + 1) * LAGS, :], (((1,), (1,)), ((), ())),
            preferred_element_type=jnp.float32,
        ) * factor
        for s in range(2):
            for h in range(2):
                result[2 * p + s, :, h * MAXLAG : (h + 1) * MAXLAG] = r[
                    h * rows : (h + 1) * rows, s * MAXLAG : (s + 1) * MAXLAG
                ]
        copy = pltpu.make_async_copy(
            result.at[2 * p : 2 * p + 2], out.at[0, 2 * p : 2 * p + 2], sem.at[p]
        )
        copy.start()
        copies.append(copy)
    for copy in copies:
        copy.wait()


def local(record, fir):
    ch, length = record.shape
    n = lax.axis_size("chan")
    vmem = pl.BlockSpec(memory_space=pltpu.VMEM)
    hbm = pl.BlockSpec(memory_space=pltpu.HBM)
    packed = ch * (SPAN // 128)
    wide, bands = pl.pallas_call(
        gather_kernel,
        out_shape=(
            pltpu.VMEM((n * ch, SPAN), jnp.float32),
            pltpu.VMEM((ch * MAXLAG, BAND), jnp.bfloat16),
        ),
        in_specs=[hbm, hbm],
        out_specs=(vmem, vmem),
        scratch_shapes=[
            pltpu.VMEM((ch, length), jnp.bfloat16),
            pltpu.VMEM(fir.shape, jnp.float32),
            pltpu.VMEM((ch, HALO), jnp.bfloat16),
            pltpu.VMEM((ch, HALO), jnp.bfloat16),
            pltpu.VMEM((packed, 128), jnp.bfloat16),
            pltpu.VMEM((n, packed, 128), jnp.bfloat16),
            pltpu.SemaphoreType.DMA((2,)),
            pltpu.SemaphoreType.DMA((2,)),
            pltpu.SemaphoreType.DMA((2,)),
            pltpu.SemaphoreType.DMA((n - 1,)),
            pltpu.SemaphoreType.DMA((n,)),
        ],
        compiler_params=pltpu.CompilerParams(
            collective_id=0, has_side_effects=True, vmem_limit_bytes=16 << 20
        ),
    )(*(pltpu.with_memory_space_constraint(x, pltpu.HBM) for x in (record, fir)))
    return pl.pallas_call(
        correlate_kernel,
        out_shape=jax.ShapeDtypeStruct((1, ch, n * ch, LAGS), jnp.float32),
        in_specs=[vmem, vmem],
        out_specs=pl.BlockSpec(memory_space=pl.ANY),
        scratch_shapes=[
            pltpu.VMEM((ch, n * ch, LAGS), jnp.float32),
            pltpu.SemaphoreType.DMA((ch // 2,)),
        ],
        compiler_params=pltpu.CompilerParams(vmem_limit_bytes=16 << 20),
    )(wide, bands)


def solution(mesh):
    in_specs = (P("chan", "tm"), P("chan", None))
    out_specs = P("tm", "chan", None, None)
    return jax.shard_map(local, mesh=mesh, in_specs=in_specs, out_specs=out_specs, check_vma=False)
```

```python
import math

import jax
import jax.numpy as jnp
from jax import lax
from jax.experimental import pallas as pl
from jax.experimental.pallas import tpu as pltpu
from jax.sharding import PartitionSpec as P

GROUP = 512
MAXLAG = 128
LAGS = 2 * MAXLAG
SPAN = GROUP + LAGS
BAND = GROUP + MAXLAG
HALO = 256
MESH = pl.DeviceIdType.MESH


def whiten(x, taps, width, length):
    count = taps.shape[1]
    x = x[:, :width]
    steps = 8
    moved = [x if b == 0 else pltpu.roll(x, width - b, 1) for b in range(steps)]
    total = None
    for a in range(0, count, steps):
        part = None
        for b in range(min(steps, count - a)):
            term = taps[:, a + b : a + b + 1] * moved[b]
            part = term if part is None else part + term
        if a:
            part = pltpu.roll(part, width - a, 1)
        total = part if total is None else total + part
    return total[:, :length]


def pack(y):
    return jnp.concatenate(
        [y[:, k : k + 128] for k in range(0, y.shape[1], 128)], axis=0
    ).astype(jnp.bfloat16)


def gather_kernel(record_hbm, fir_hbm, wide, bands, record, fir, low, high, own, blocks,
                  load, halo_send, halo_recv, send, recv, near, ready):
    n, tn = lax.axis_size("chan"), lax.axis_size("tm")
    me, tm = lax.axis_index("chan"), lax.axis_index("tm")
    ch, length = record.shape

    first, last = tm == 0, tm == tn - 1

    barrier = pltpu.get_barrier_semaphore()
    for c in range(1, n):
        @pl.when(me < c)
        def _():
            pl.semaphore_signal(barrier, inc=1, device_id=(c, tm), device_id_type=MESH)

    @pl.when(jnp.logical_not(last))
    def _():
        pl.semaphore_signal(barrier, inc=1, device_id=(me, tm + 1), device_id_type=MESH)

    get_record = pltpu.make_async_copy(record_hbm, record, load.at[0])
    get_fir = pltpu.make_async_copy(fir_hbm, fir, load.at[1])
    get_record.start()
    get_fir.start()
    earlier = me + jnp.minimum(tm, 1)

    @pl.when(earlier > 0)
    def _():
        pl.semaphore_wait(barrier, earlier)

    @pl.when(jnp.logical_not(first))
    def _():
        pl.semaphore_signal(near, inc=1, device_id=(me, tm - 1), device_id_type=MESH)

    get_record.wait()
    to_left = pltpu.make_async_remote_copy(
        record.at[:, :HALO], high, halo_send.at[1], halo_recv.at[1],
        device_id=(me, jnp.maximum(tm - 1, 0)), device_id_type=MESH,
    )
    to_right = pltpu.make_async_remote_copy(
        record.at[:, length - HALO :], low, halo_send.at[0], halo_recv.at[0],
        device_id=(me, jnp.minimum(tm + 1, tn - 1)), device_id_type=MESH,
    )

    @pl.when(jnp.logical_not(first))
    def _():
        to_left.start()

    for c in range(n - 1):
        @pl.when(me > c)
        def _():
            pl.semaphore_signal(ready.at[me], inc=1, device_id=(c, tm), device_id_type=MESH)

    @pl.when(jnp.logical_not(last))
    def _():
        pl.semaphore_wait(near, 1)
        to_right.start()

    get_fir.wait()

    @pl.when(first)
    def _():
        low[...] = jnp.zeros_like(low)

    @pl.when(last)
    def _():
        high[...] = jnp.zeros_like(high)

    half = (fir.shape[1] - 1) // 2
    edge = MAXLAG + half
    taps = fir[...]
    x = record[...].astype(jnp.float32)
    x = jnp.concatenate([jnp.zeros((ch, HALO), jnp.float32), x, jnp.zeros((ch, HALO), jnp.float32)], axis=1)
    y = whiten(pltpu.roll(x, x.shape[1] - (HALO - edge), 1), taps, SPAN + 128, SPAN)

    @pl.when(jnp.logical_not(last))
    def _():
        to_left.wait_recv()

    @pl.when(jnp.logical_not(first))
    def _():
        to_right.wait_recv()

    column = lax.broadcasted_iota(jnp.int32, (ch, HALO), 1)
    x = pltpu.roll(low[...].astype(jnp.float32), edge, 1)
    x = jnp.where(column < edge, x, 0.0)
    before = jnp.where(column < edge, whiten(x, taps, HALO, HALO), 0.0)
    x = pltpu.roll(high[...].astype(jnp.float32), 2 * half, 1)
    x = jnp.where((column >= 2 * half) & (column < 2 * half + edge), x, 0.0)
    after = jnp.where(column < edge, whiten(x, taps, HALO, HALO), 0.0)
    after = pltpu.roll(after, HALO - edge, 1)
    y = jnp.concatenate(
        [y[:, :HALO] + before, y[:, HALO : SPAN - HALO], y[:, SPAN - HALO :] + after], axis=1
    )
    at = lax.broadcasted_iota(jnp.int32, y.shape, 1) + (tm * GROUP - MAXLAG)
    y = jnp.where((at >= 0) & (at < tn * GROUP), y, 0.0)
    y = y.astype(jnp.bfloat16).astype(jnp.float32)
    own[...] = pack(y)

    copies = [
        pltpu.make_async_remote_copy(
            own, blocks.at[me], send.at[c], recv.at[me],
            device_id=(c, tm), device_id_type=MESH,
        )
        for c in range(n)
    ]
    for c in range(n - 1):
        @pl.when(me > c)
        def _():
            copies[c].start()
    blocks[me] = own[...]

    lead = jnp.concatenate(
        [y[:, MAXLAG : MAXLAG + GROUP], jnp.zeros((ch, MAXLAG), jnp.float32)], axis=1
    )
    for i in range(ch):
        line = jnp.broadcast_to(lead[i : i + 1, :], (MAXLAG, BAND))
        moved = pltpu.roll(line, 0, 1, stride=1, stride_axis=0)
        bands[i * MAXLAG : (i + 1) * MAXLAG, :] = moved.astype(jnp.bfloat16)

    for c in range(1, n):
        @pl.when(me < c)
        def _():
            pl.semaphore_wait(ready.at[c], 1)
            copies[c].start()

    for c in range(n):
        @pl.when(me != c)
        def _():
            pltpu.make_async_remote_copy(
                own, blocks.at[c], send.at[c], recv.at[c],
                device_id=(c, tm), device_id_type=MESH,
            ).wait_recv()

        block = blocks[c].astype(jnp.float32)
        for k in range(SPAN // 128):
            wide[c * ch : (c + 1) * ch, k * 128 : (k + 1) * 128] = block[k * ch : (k + 1) * ch, :]

    @pl.when(jnp.logical_not(first))
    def _():
        to_left.wait_send()

    @pl.when(jnp.logical_not(last))
    def _():
        to_right.wait_send()

    for c in range(n):
        @pl.when(me != c)
        def _():
            copies[c].wait_send()


def correlate_kernel(wide, bands, out, result, sem):
    rows = wide.shape[0]
    ch = bands.shape[0] // MAXLAG
    factor = 1.0 / math.sqrt(GROUP)
    w = wide[...].astype(jnp.bfloat16)
    both = jnp.concatenate([w[:, :BAND], w[:, MAXLAG:]], axis=0)
    copies = []
    for p in range(ch // 2):
        r = lax.dot_general(
            both, bands[p * LAGS : (p + 1) * LAGS, :], (((1,), (1,)), ((), ())),
            preferred_element_type=jnp.float32,
        ) * factor
        for s in range(2):
            for h in range(2):
                result[2 * p + s, :, h * MAXLAG : (h + 1) * MAXLAG] = r[
                    h * rows : (h + 1) * rows, s * MAXLAG : (s + 1) * MAXLAG
                ]
        copy = pltpu.make_async_copy(
            result.at[2 * p : 2 * p + 2], out.at[0, 2 * p : 2 * p + 2], sem.at[p]
        )
        copy.start()
        copies.append(copy)
    for copy in copies:
        copy.wait()


def local(record, fir):
    ch, length = record.shape
    n = lax.axis_size("chan")
    vmem = pl.BlockSpec(memory_space=pltpu.VMEM)
    hbm = pl.BlockSpec(memory_space=pltpu.HBM)
    packed = ch * (SPAN // 128)
    wide, bands = pl.pallas_call(
        gather_kernel,
        out_shape=(
            pltpu.VMEM((n * ch, SPAN), jnp.float32),
            pltpu.VMEM((ch * MAXLAG, BAND), jnp.bfloat16),
        ),
        in_specs=[hbm, hbm],
        out_specs=(vmem, vmem),
        scratch_shapes=[
            pltpu.VMEM((ch, length), jnp.bfloat16),
            pltpu.VMEM(fir.shape, jnp.float32),
            pltpu.VMEM((ch, HALO), jnp.bfloat16),
            pltpu.VMEM((ch, HALO), jnp.bfloat16),
            pltpu.VMEM((packed, 128), jnp.bfloat16),
            pltpu.VMEM((n, packed, 128), jnp.bfloat16),
            pltpu.SemaphoreType.DMA((2,)),
            pltpu.SemaphoreType.DMA((2,)),
            pltpu.SemaphoreType.DMA((2,)),
            pltpu.SemaphoreType.DMA((n,)),
            pltpu.SemaphoreType.DMA((n,)),
            pltpu.SemaphoreType.REGULAR,
            pltpu.SemaphoreType.REGULAR((n,)),
        ],
        compiler_params=pltpu.CompilerParams(
            collective_id=0, has_side_effects=True, vmem_limit_bytes=16 << 20
        ),
    )(*(pltpu.with_memory_space_constraint(x, pltpu.HBM) for x in (record, fir)))
    return pl.pallas_call(
        correlate_kernel,
        out_shape=jax.ShapeDtypeStruct((1, ch, n * ch, LAGS), jnp.float32),
        in_specs=[vmem, vmem],
        out_specs=pl.BlockSpec(memory_space=pl.ANY),
        scratch_shapes=[
            pltpu.VMEM((ch, n * ch, LAGS), jnp.float32),
            pltpu.SemaphoreType.DMA((ch // 2,)),
        ],
        compiler_params=pltpu.CompilerParams(vmem_limit_bytes=16 << 20),
    )(wide, bands)


def solution(mesh):
    in_specs = (P("chan", "tm"), P("chan", None))
    out_specs = P("tm", "chan", None, None)
    return jax.shard_map(local, mesh=mesh, in_specs=in_specs, out_specs=out_specs, check_vma=False)
```

```python
import math

import jax
import jax.numpy as jnp
from jax import lax
from jax.experimental import pallas as pl
from jax.experimental.pallas import tpu as pltpu
from jax.sharding import PartitionSpec as P

GROUP = 512
MAXLAG = 128
LAGS = 2 * MAXLAG
SPAN = GROUP + LAGS
BAND = GROUP + MAXLAG
HALO = 256
MESH = pl.DeviceIdType.MESH


def whiten(x, taps, width, length):
    count = taps.shape[1]
    x = x[:, :width]
    steps = 8
    moved = [x if b == 0 else pltpu.roll(x, width - b, 1) for b in range(steps)]
    total = None
    for a in range(0, count, steps):
        part = None
        for b in range(min(steps, count - a)):
            term = taps[:, a + b : a + b + 1] * moved[b]
            part = term if part is None else part + term
        if a:
            part = pltpu.roll(part, width - a, 1)
        total = part if total is None else total + part
    return total[:, :length]


def pack(y):
    return jnp.concatenate(
        [y[:, k : k + 128] for k in range(0, y.shape[1], 128)], axis=0
    ).astype(jnp.bfloat16)


def gather_kernel(record_hbm, fir_hbm, wide, bands, record, fir, low, high, own, blocks,
                  load, halo_send, halo_recv, send, recv, near, ready):
    n, tn = lax.axis_size("chan"), lax.axis_size("tm")
    me, tm = lax.axis_index("chan"), lax.axis_index("tm")
    ch, length = record.shape

    first, last = tm == 0, tm == tn - 1

    barrier = pltpu.get_barrier_semaphore()
    for c in range(1, n):
        @pl.when(me < c)
        def _():
            pl.semaphore_signal(barrier, inc=1, device_id=(c, tm), device_id_type=MESH)

    @pl.when(jnp.logical_not(last))
    def _():
        pl.semaphore_signal(barrier, inc=1, device_id=(me, tm + 1), device_id_type=MESH)

    get_record = pltpu.make_async_copy(record_hbm, record, load.at[0])
    get_fir = pltpu.make_async_copy(fir_hbm, fir, load.at[1])
    get_record.start()
    get_fir.start()
    earlier = me + jnp.minimum(tm, 1)

    @pl.when(earlier > 0)
    def _():
        pl.semaphore_wait(barrier, earlier)

    @pl.when(jnp.logical_not(first))
    def _():
        pl.semaphore_signal(near, inc=1, device_id=(me, tm - 1), device_id_type=MESH)

    get_record.wait()
    to_left = pltpu.make_async_remote_copy(
        record.at[:, :HALO], high, halo_send.at[1], halo_recv.at[1],
        device_id=(me, jnp.maximum(tm - 1, 0)), device_id_type=MESH,
    )
    to_right = pltpu.make_async_remote_copy(
        record.at[:, length - HALO :], low, halo_send.at[0], halo_recv.at[0],
        device_id=(me, jnp.minimum(tm + 1, tn - 1)), device_id_type=MESH,
    )

    @pl.when(jnp.logical_not(first))
    def _():
        to_left.start()

    for c in range(n - 1):
        @pl.when(me > c)
        def _():
            pl.semaphore_signal(ready.at[me], inc=1, device_id=(c, tm), device_id_type=MESH)

    @pl.when(jnp.logical_not(last))
    def _():
        pl.semaphore_wait(near, 1)
        to_right.start()

    get_fir.wait()

    @pl.when(first)
    def _():
        low[...] = jnp.zeros_like(low)

    @pl.when(last)
    def _():
        high[...] = jnp.zeros_like(high)

    half = (fir.shape[1] - 1) // 2
    edge = MAXLAG + half
    taps = fir[...]
    x = record[...].astype(jnp.float32)
    x = jnp.concatenate([x, jnp.zeros((ch, MAXLAG), jnp.float32)], axis=1)
    y = whiten(pltpu.roll(x, 2 * half, 1), taps, BAND, BAND)
    y = jnp.concatenate([y, jnp.zeros((ch, MAXLAG), jnp.float32)], axis=1)
    y = pltpu.roll(y, MAXLAG - half, 1)

    @pl.when(jnp.logical_not(last))
    def _():
        to_left.wait_recv()

    @pl.when(jnp.logical_not(first))
    def _():
        to_right.wait_recv()

    column = lax.broadcasted_iota(jnp.int32, (ch, HALO), 1)
    x = pltpu.roll(low[...].astype(jnp.float32), edge, 1)
    x = jnp.where(column < edge, x, 0.0)
    before = jnp.where(column < edge, whiten(x, taps, HALO, HALO), 0.0)
    x = pltpu.roll(high[...].astype(jnp.float32), 2 * half, 1)
    x = jnp.where((column >= 2 * half) & (column < 2 * half + edge), x, 0.0)
    after = jnp.where(column < edge, whiten(x, taps, HALO, HALO), 0.0)
    after = pltpu.roll(after, HALO - edge, 1)
    y = jnp.concatenate(
        [y[:, :HALO] + before, y[:, HALO : SPAN - HALO], y[:, SPAN - HALO :] + after], axis=1
    )
    at = lax.broadcasted_iota(jnp.int32, y.shape, 1) + (tm * GROUP - MAXLAG)
    y = jnp.where((at >= 0) & (at < tn * GROUP), y, 0.0)
    y = y.astype(jnp.bfloat16).astype(jnp.float32)
    own[...] = pack(y)

    copies = [
        pltpu.make_async_remote_copy(
            own, blocks.at[me], send.at[c], recv.at[me],
            device_id=(c, tm), device_id_type=MESH,
        )
        for c in range(n)
    ]
    for c in range(n - 1):
        @pl.when(me > c)
        def _():
            copies[c].start()
    blocks[me] = own[...]

    lead = jnp.concatenate(
        [y[:, MAXLAG : MAXLAG + GROUP], jnp.zeros((ch, MAXLAG), jnp.float32)], axis=1
    )
    for i in range(ch):
        line = jnp.broadcast_to(lead[i : i + 1, :], (MAXLAG, BAND))
        moved = pltpu.roll(line, 0, 1, stride=1, stride_axis=0)
        bands[i * MAXLAG : (i + 1) * MAXLAG, :] = moved.astype(jnp.bfloat16)

    for c in range(1, n):
        @pl.when(me < c)
        def _():
            pl.semaphore_wait(ready.at[c], 1)
            copies[c].start()

    for c in range(n):
        @pl.when(me != c)
        def _():
            pltpu.make_async_remote_copy(
                own, blocks.at[c], send.at[c], recv.at[c],
                device_id=(c, tm), device_id_type=MESH,
            ).wait_recv()

        block = blocks[c].astype(jnp.float32)
        for k in range(SPAN // 128):
            wide[c * ch : (c + 1) * ch, k * 128 : (k + 1) * 128] = block[k * ch : (k + 1) * ch, :]

    @pl.when(jnp.logical_not(first))
    def _():
        to_left.wait_send()

    @pl.when(jnp.logical_not(last))
    def _():
        to_right.wait_send()

    for c in range(n):
        @pl.when(me != c)
        def _():
            copies[c].wait_send()


def correlate_kernel(wide, bands, out, result, sem):
    rows = wide.shape[0]
    ch = bands.shape[0] // MAXLAG
    factor = 1.0 / math.sqrt(GROUP)
    w = wide[...].astype(jnp.bfloat16)
    both = jnp.concatenate([w[:, :BAND], w[:, MAXLAG:]], axis=0)
    copies = []
    for p in range(ch // 2):
        r = lax.dot_general(
            both, bands[p * LAGS : (p + 1) * LAGS, :], (((1,), (1,)), ((), ())),
            preferred_element_type=jnp.float32,
        ) * factor
        for s in range(2):
            for h in range(2):
                result[2 * p + s, :, h * MAXLAG : (h + 1) * MAXLAG] = r[
                    h * rows : (h + 1) * rows, s * MAXLAG : (s + 1) * MAXLAG
                ]
            copy = pltpu.make_async_copy(
                result.at[2 * p + s], out.at[0, 2 * p + s], sem.at[2 * p + s]
            )
            copy.start()
            copies.append(copy)
    for copy in copies:
        copy.wait()


def local(record, fir):
    ch, length = record.shape
    n = lax.axis_size("chan")
    vmem = pl.BlockSpec(memory_space=pltpu.VMEM)
    hbm = pl.BlockSpec(memory_space=pltpu.HBM)
    packed = ch * (SPAN // 128)
    wide, bands = pl.pallas_call(
        gather_kernel,
        out_shape=(
            pltpu.VMEM((n * ch, SPAN), jnp.float32),
            pltpu.VMEM((ch * MAXLAG, BAND), jnp.bfloat16),
        ),
        in_specs=[hbm, hbm],
        out_specs=(vmem, vmem),
        scratch_shapes=[
            pltpu.VMEM((ch, length), jnp.bfloat16),
            pltpu.VMEM(fir.shape, jnp.float32),
            pltpu.VMEM((ch, HALO), jnp.bfloat16),
            pltpu.VMEM((ch, HALO), jnp.bfloat16),
            pltpu.VMEM((packed, 128), jnp.bfloat16),
            pltpu.VMEM((n, packed, 128), jnp.bfloat16),
            pltpu.SemaphoreType.DMA((2,)),
            pltpu.SemaphoreType.DMA((2,)),
            pltpu.SemaphoreType.DMA((2,)),
            pltpu.SemaphoreType.DMA((n,)),
            pltpu.SemaphoreType.DMA((n,)),
            pltpu.SemaphoreType.REGULAR,
            pltpu.SemaphoreType.REGULAR((n,)),
        ],
        compiler_params=pltpu.CompilerParams(
            collective_id=0, has_side_effects=True, vmem_limit_bytes=16 << 20
        ),
    )(*(pltpu.with_memory_space_constraint(x, pltpu.HBM) for x in (record, fir)))
    return pl.pallas_call(
        correlate_kernel,
        out_shape=jax.ShapeDtypeStruct((1, ch, n * ch, LAGS), jnp.float32),
        in_specs=[vmem, vmem],
        out_specs=pl.BlockSpec(memory_space=pl.ANY),
        scratch_shapes=[
            pltpu.VMEM((ch, n * ch, LAGS), jnp.float32),
            pltpu.SemaphoreType.DMA((ch,)),
        ],
        compiler_params=pltpu.CompilerParams(vmem_limit_bytes=16 << 20),
    )(wide, bands)


def solution(mesh):
    in_specs = (P("chan", "tm"), P("chan", None))
    out_specs = P("tm", "chan", None, None)
    return jax.shard_map(local, mesh=mesh, in_specs=in_specs, out_specs=out_specs, check_vma=False)
```

```python
import math

import jax
import jax.numpy as jnp
from jax import lax
from jax.experimental import pallas as pl
from jax.experimental.pallas import tpu as pltpu
from jax.sharding import PartitionSpec as P

GROUP = 512
MAXLAG = 128
LAGS = 2 * MAXLAG
SPAN = GROUP + LAGS
BAND = GROUP + MAXLAG
HALO = 256
MESH = pl.DeviceIdType.MESH


def whiten(x, taps, width, length):
    count = taps.shape[1]
    x = x[:, :width]
    steps = 8
    moved = [x if b == 0 else pltpu.roll(x, width - b, 1) for b in range(steps)]
    total = None
    for a in range(0, count, steps):
        part = None
        for b in range(min(steps, count - a)):
            term = taps[:, a + b : a + b + 1] * moved[b]
            part = term if part is None else part + term
        if a:
            part = pltpu.roll(part, width - a, 1)
        total = part if total is None else total + part
    return total[:, :length]


def pack(y):
    return jnp.concatenate(
        [y[:, k : k + 128] for k in range(0, y.shape[1], 128)], axis=0
    ).astype(jnp.bfloat16)


def gather_kernel(record_hbm, fir_hbm, wide, bands, record, fir, low, high, own, blocks,
                  load, halo_send, halo_recv, send, recv, near, ready):
    n, tn = lax.axis_size("chan"), lax.axis_size("tm")
    me, tm = lax.axis_index("chan"), lax.axis_index("tm")
    ch, length = record.shape

    first, last = tm == 0, tm == tn - 1

    barrier = pltpu.get_barrier_semaphore()
    get_record = pltpu.make_async_copy(record_hbm, record, load.at[0])
    get_fir = pltpu.make_async_copy(fir_hbm, fir, load.at[1])
    get_record.start()
    get_fir.start()
    for c in range(1, n):
        @pl.when(me < c)
        def _():
            pl.semaphore_signal(barrier, inc=1, device_id=(c, tm), device_id_type=MESH)

    @pl.when(jnp.logical_not(last))
    def _():
        pl.semaphore_signal(barrier, inc=1, device_id=(me, tm + 1), device_id_type=MESH)

    earlier = me + jnp.minimum(tm, 1)

    @pl.when(earlier > 0)
    def _():
        pl.semaphore_wait(barrier, earlier)

    @pl.when(jnp.logical_not(first))
    def _():
        pl.semaphore_signal(near, inc=1, device_id=(me, tm - 1), device_id_type=MESH)

    for c in range(n - 1):
        @pl.when(me > c)
        def _():
            pl.semaphore_signal(ready.at[me], inc=1, device_id=(c, tm), device_id_type=MESH)

    get_record.wait()
    to_left = pltpu.make_async_remote_copy(
        record.at[:, :HALO], high, halo_send.at[1], halo_recv.at[1],
        device_id=(me, jnp.maximum(tm - 1, 0)), device_id_type=MESH,
    )
    to_right = pltpu.make_async_remote_copy(
        record.at[:, length - HALO :], low, halo_send.at[0], halo_recv.at[0],
        device_id=(me, jnp.minimum(tm + 1, tn - 1)), device_id_type=MESH,
    )

    @pl.when(jnp.logical_not(first))
    def _():
        to_left.start()

    @pl.when(jnp.logical_not(last))
    def _():
        pl.semaphore_wait(near, 1)
        to_right.start()

    get_fir.wait()

    @pl.when(first)
    def _():
        low[...] = jnp.zeros_like(low)

    @pl.when(last)
    def _():
        high[...] = jnp.zeros_like(high)

    half = (fir.shape[1] - 1) // 2
    edge = MAXLAG + half
    taps = fir[...]
    x = record[...].astype(jnp.float32)
    x = jnp.concatenate([x, jnp.zeros((ch, MAXLAG), jnp.float32)], axis=1)
    y = whiten(pltpu.roll(x, 2 * half, 1), taps, BAND, BAND)
    y = jnp.concatenate([y, jnp.zeros((ch, MAXLAG), jnp.float32)], axis=1)
    y = pltpu.roll(y, MAXLAG - half, 1)

    @pl.when(jnp.logical_not(last))
    def _():
        to_left.wait_recv()

    @pl.when(jnp.logical_not(first))
    def _():
        to_right.wait_recv()

    column = lax.broadcasted_iota(jnp.int32, (ch, HALO), 1)
    x = pltpu.roll(low[...].astype(jnp.float32), edge, 1)
    x = jnp.where(column < edge, x, 0.0)
    before = jnp.where(column < edge, whiten(x, taps, HALO, HALO), 0.0)
    x = pltpu.roll(high[...].astype(jnp.float32), 2 * half, 1)
    x = jnp.where((column >= 2 * half) & (column < 2 * half + edge), x, 0.0)
    after = jnp.where(column < edge, whiten(x, taps, HALO, HALO), 0.0)
    after = pltpu.roll(after, HALO - edge, 1)
    y = jnp.concatenate(
        [y[:, :HALO] + before, y[:, HALO : SPAN - HALO], y[:, SPAN - HALO :] + after], axis=1
    )
    at = lax.broadcasted_iota(jnp.int32, y.shape, 1) + (tm * GROUP - MAXLAG)
    y = jnp.where((at >= 0) & (at < tn * GROUP), y, 0.0)
    y = y.astype(jnp.bfloat16).astype(jnp.float32)
    own[...] = pack(y)

    copies = [
        pltpu.make_async_remote_copy(
            own, blocks.at[me], send.at[c], recv.at[me],
            device_id=(c, tm), device_id_type=MESH,
        )
        for c in range(n)
    ]
    for c in range(n - 1):
        @pl.when(me > c)
        def _():
            copies[c].start()
    blocks[me] = own[...]

    lead = jnp.concatenate(
        [y[:, MAXLAG : MAXLAG + GROUP], jnp.zeros((ch, MAXLAG), jnp.float32)], axis=1
    )
    for i in range(ch):
        line = jnp.broadcast_to(lead[i : i + 1, :], (MAXLAG, BAND))
        moved = pltpu.roll(line, 0, 1, stride=1, stride_axis=0)
        bands[i * MAXLAG : (i + 1) * MAXLAG, :] = moved.astype(jnp.bfloat16)

    for c in range(1, n):
        @pl.when(me < c)
        def _():
            pl.semaphore_wait(ready.at[c], 1)
            copies[c].start()

    for c in range(n):
        @pl.when(me != c)
        def _():
            pltpu.make_async_remote_copy(
                own, blocks.at[c], send.at[c], recv.at[c],
                device_id=(c, tm), device_id_type=MESH,
            ).wait_recv()

        block = blocks[c].astype(jnp.float32)
        for k in range(SPAN // 128):
            wide[c * ch : (c + 1) * ch, k * 128 : (k + 1) * 128] = block[k * ch : (k + 1) * ch, :]

    @pl.when(jnp.logical_not(first))
    def _():
        to_left.wait_send()

    @pl.when(jnp.logical_not(last))
    def _():
        to_right.wait_send()

    for c in range(n):
        @pl.when(me != c)
        def _():
            copies[c].wait_send()


def correlate_kernel(wide, bands, out, result, sem):
    rows = wide.shape[0]
    ch = bands.shape[0] // MAXLAG
    factor = 1.0 / math.sqrt(GROUP)
    w = wide[...].astype(jnp.bfloat16)
    both = jnp.concatenate([w[:, :BAND], w[:, MAXLAG:]], axis=0)
    copies = []
    for p in range(ch // 2):
        r = lax.dot_general(
            both, bands[p * LAGS : (p + 1) * LAGS, :], (((1,), (1,)), ((), ())),
            preferred_element_type=jnp.float32,
        ) * factor
        for s in range(2):
            for h in range(2):
                result[2 * p + s, :, h * MAXLAG : (h + 1) * MAXLAG] = r[
                    h * rows : (h + 1) * rows, s * MAXLAG : (s + 1) * MAXLAG
                ]
            copy = pltpu.make_async_copy(
                result.at[2 * p + s], out.at[0, 2 * p + s], sem.at[2 * p + s]
            )
            copy.start()
            copies.append(copy)
    for copy in copies:
        copy.wait()


def local(record, fir):
    ch, length = record.shape
    n = lax.axis_size("chan")
    vmem = pl.BlockSpec(memory_space=pltpu.VMEM)
    hbm = pl.BlockSpec(memory_space=pltpu.HBM)
    packed = ch * (SPAN // 128)
    wide, bands = pl.pallas_call(
        gather_kernel,
        out_shape=(
            pltpu.VMEM((n * ch, SPAN), jnp.float32),
            pltpu.VMEM((ch * MAXLAG, BAND), jnp.bfloat16),
        ),
        in_specs=[hbm, hbm],
        out_specs=(vmem, vmem),
        scratch_shapes=[
            pltpu.VMEM((ch, length), jnp.bfloat16),
            pltpu.VMEM(fir.shape, jnp.float32),
            pltpu.VMEM((ch, HALO), jnp.bfloat16),
            pltpu.VMEM((ch, HALO), jnp.bfloat16),
            pltpu.VMEM((packed, 128), jnp.bfloat16),
            pltpu.VMEM((n, packed, 128), jnp.bfloat16),
            pltpu.SemaphoreType.DMA((2,)),
            pltpu.SemaphoreType.DMA((2,)),
            pltpu.SemaphoreType.DMA((2,)),
            pltpu.SemaphoreType.DMA((n,)),
            pltpu.SemaphoreType.DMA((n,)),
            pltpu.SemaphoreType.REGULAR,
            pltpu.SemaphoreType.REGULAR((n,)),
        ],
        compiler_params=pltpu.CompilerParams(
            collective_id=0, has_side_effects=True, vmem_limit_bytes=16 << 20
        ),
    )(*(pltpu.with_memory_space_constraint(x, pltpu.HBM) for x in (record, fir)))
    return pl.pallas_call(
        correlate_kernel,
        out_shape=jax.ShapeDtypeStruct((1, ch, n * ch, LAGS), jnp.float32),
        in_specs=[vmem, vmem],
        out_specs=pl.BlockSpec(memory_space=pl.ANY),
        scratch_shapes=[
            pltpu.VMEM((ch, n * ch, LAGS), jnp.float32),
            pltpu.SemaphoreType.DMA((ch,)),
        ],
        compiler_params=pltpu.CompilerParams(vmem_limit_bytes=16 << 20),
    )(wide, bands)


def solution(mesh):
    in_specs = (P("chan", "tm"), P("chan", None))
    out_specs = P("tm", "chan", None, None)
    return jax.shard_map(local, mesh=mesh, in_specs=in_specs, out_specs=out_specs, check_vma=False)
```
